32 devices in a mesh: rows: 4 (over y, core), dp: 8 (over z, x).
Axes of the slice: x: 2, y: 2, z: 4, core: 2. Of those that a mesh axis runs over, the one named last changes fastest.
Arguments:
- emb_weight: float32 [8, 6144, 128], P('dp', 'rows'), may hold values from -160 to 160
- emb_grad: bfloat16 [8, 6144, 128], P('dp', 'rows'), may hold values from -6 to 6
- emb_moment: float32 [8, 6144, 128], P('dp', 'rows'), may hold values from -160 to 160
- emb_second: float32 [8, 6144, 128], P('dp', 'rows'), may hold values from 0.1 to 4
- hot_rows: int32 [8, 4, 256], P('dp', 'rows'), may hold values from 0 to 1535
- block_counts: int32 [8, 4], P('dp', 'rows'), may hold values from 1 to 2, as said below
- dense_weight: float32 [512, 256], replicated, may hold values from -8 to 8
- dense_grad: float32 [32, 512, 256], P(('rows', 'dp')), may hold values from -6 to 6
- dense_moment: float32 [512, 256], replicated, may hold values from -900 to 900
- dense_second: float32 [512, 256], replicated, may hold values from 3.2 to 128
Outputs:
- new_weight: float32 [8, 6144, 128], P('dp', 'rows')
- new_moment: float32 [8, 6144, 128], P('dp', 'rows')
- new_second: float32 [8, 6144, 128], P('dp', 'rows')
- hot_cache: bfloat16 [8, 4, 256, 128], P(None, 'rows')
- fresh_dense: float32 [512, 256], replicated
- fresh_moment: float32 [512, 256], replicated
- fresh_second: float32 [512, 256], replicated
The draws below stay inside these ranges and needn't reach their ends.
Inputs may be any that keep to these rules, and one draw needn't show every extreme that they name: `block_counts`: some table shard has 2 live blocks in every draw. `hot_rows`: entries in dead blocks are ignored.
All inputs are finite; a program needn't handle non-finite values.
Results may differ from the reference program's by a relative error of at most 0.001.
Values may be sent and summed in bfloat16 or wider, within the bound.
A program may use at most 64 MiB of HBM per device.

```python
import math
import jax
import jax.numpy as jnp
from jax import lax

E = 128
DIN = 512
DOUT = 256
RS = 1536
BLOCK = 128
HB = 2
TABLES = 8
TROWS = 6144
N_ROWS = 4
N_DP = 8


def scaled_field(key, lead, height, width, base_scale, ramped):
    base_key, row_key, col_key = jax.random.split(jax.random.fold_in(key, 11), 3)
    base = jnp.clip(jax.random.normal(base_key, (lead, height, width), jnp.float32), -6.0, 6.0)
    top_ratio = 3.0
    row_scale = jnp.exp(jax.random.uniform(row_key, (lead, height, 1), jnp.float32, math.log(0.3), math.log(3.0)))
    col_scale = jnp.exp(jax.random.uniform(col_key, (lead, 1, width), jnp.float32, math.log(0.3), math.log(3.0)))
    field = base * row_scale * col_scale * base_scale
    if ramped:
        position = jnp.arange(height, dtype=jnp.float32) / (height - 1)
        field = field * jnp.sqrt(1.0 + (top_ratio - 1.0) * position)[None, :, None]
    return field


def draw_emb_weight(key, part):
    return scaled_field(jax.random.fold_in(key, 101), TABLES, TROWS, E, 1.0, True)


def draw_emb_moment(key, part):
    return scaled_field(jax.random.fold_in(key, 202), TABLES, TROWS, E, 1.0, True)


def draw_dense_weight(key, part):
    return scaled_field(jax.random.fold_in(key, 303), 1, DIN, DOUT, DIN ** (-0.5), False)[0]


def draw_dense_moment(key, part):
    return scaled_field(jax.random.fold_in(key, 404), 1, DIN, DOUT, (TROWS // RS * TABLES) ** 0.5, False)[0]


def draw_block_counts(key, part):
    shard_count = TROWS // RS
    count_key, spot_key = jax.random.split(jax.random.fold_in(key, 23))
    counts = jax.random.randint(count_key, (TABLES * shard_count,), 1, HB + 1, dtype=jnp.int32)
    spot_index = jax.random.randint(spot_key, (), 0, TABLES * shard_count, dtype=jnp.int32)
    counts = counts.at[spot_index].set(HB)
    return counts.reshape(TABLES, shard_count)


def set_ends(result, stream_key, least, largest):
    longest = result.shape.index(max(result.shape))
    spots = []
    for shift in (0, 1):
        where = [jax.random.randint(jax.random.fold_in(stream_key, axis), (), 0, length) for axis, length in enumerate(result.shape)]
        where[longest] = (where[longest] + shift) % result.shape[longest]
        spots.append(tuple(where))
    return result.at[spots[0]].set(least).at[spots[1]].set(largest)


def block_levels(key, shape, cuts, least, top_value):
    factor_of = 1.0
    for dim, blocks in cuts:
        heights = jax.random.uniform(jax.random.fold_in(jax.random.fold_in(key, 6), dim), (blocks,), jnp.float32, least / len(cuts), top_value / len(cuts))
        factor_of = factor_of * jnp.repeat(jnp.exp(heights), shape[dim] // blocks).reshape((-1,) + (1,) * (len(shape) - 1 - dim))
    return factor_of


def bell_draw(stream_key, shape, spread, bound, pieces=(), kind=jnp.bfloat16):
    entries = spread * jax.random.normal(stream_key, shape, jnp.float32)
    if pieces:
        entries = entries * block_levels(stream_key, shape, pieces, -0.22, 0.18)
    return jnp.clip(entries, -bound, bound).astype(kind)


def setup_inputs(seed: int = 0) -> dict:
    seeds = jax.random.split(jax.random.key(seed), 11)
    return {
        "emb_weight": draw_emb_weight(jax.random.fold_in(seeds[10], 71), 0),
        "emb_grad": bell_draw(seeds[1], (TABLES, TROWS, E), 1.0, 6.0, ((0, 8), (1, 4))),
        "emb_moment": draw_emb_moment(jax.random.fold_in(seeds[10], 71), 0),
        "emb_second": jnp.clip(jnp.exp(math.log(4.0) - 3.6888794 * jax.random.uniform(seeds[3], (TABLES, TROWS, E), jnp.float32) ** block_levels(seeds[3], (TABLES, TROWS, E), ((0, 8), (1, 4)), -0.2, 0.2)), 0.1, 4.0),
        "hot_rows": set_ends(jax.random.randint(seeds[4], (TABLES, N_ROWS, HB * BLOCK), 0, RS), jax.random.fold_in(seeds[4], 1), 0, RS - 1).astype(jnp.int32),
        "block_counts": draw_block_counts(jax.random.fold_in(seeds[10], 71), 0),
        "dense_weight": draw_dense_weight(jax.random.fold_in(seeds[10], 71), 0),
        "dense_grad": bell_draw(seeds[7], (N_ROWS * N_DP, DIN, DOUT), 1.0, 6.0, ((0, 32),), jnp.float32),
        "dense_moment": draw_dense_moment(jax.random.fold_in(seeds[10], 71), 0),
        "dense_second": jnp.clip(jnp.exp(jax.random.uniform(seeds[9], (DIN, DOUT), jnp.float32, math.log(3.2), math.log(128.0))), 3.2, 128.0),
    }


beta_one = 0.9
beta_two = 0.999
first_fix = 1.0 / (1.0 - 0.9 ** 10)
second_fix = 1.0 / (1.0 - 0.999 ** 10)
epsilon = 1e-06
norm_floor = 1e-06
decay_rate = 0.1
learn_rate = 0.05

def moments(weight, gradient, moment, second):
    new_moment = beta_one * moment + (1.0 - beta_one) * gradient
    new_second = beta_two * second + (1.0 - beta_two) * gradient * gradient
    direction = first_fix * new_moment / (jnp.sqrt(second_fix * new_second) + epsilon)
    return (new_moment, new_second, direction)

def trust_step(weight_sq, update_sq):
    return learn_rate * jnp.sqrt(weight_sq + norm_floor) / jnp.sqrt(update_sq + norm_floor)

def one_table(packed):
    weight, gradient, moment, second, row_ids, counts = packed
    new_moment, new_second, direction = moments(weight, gradient.astype(jnp.float32), moment, second)
    update = direction + decay_rate * weight
    step_size = trust_step(jnp.sum(weight * weight), jnp.sum(update * update))
    new_weight = weight - step_size * update
    shards = new_weight.reshape(row_ids.shape[0], -1, new_weight.shape[-1])
    picked = jnp.take_along_axis(shards, row_ids[:, :, None], axis=1)
    live_mask = jnp.arange(row_ids.shape[1], dtype=jnp.int32)[None, :] < BLOCK * counts[:, None]
    cached = jnp.where(live_mask[:, :, None], picked, jnp.zeros_like(picked)).astype(jnp.bfloat16)
    return (new_weight, new_moment, new_second, cached)

def reference(emb_weight, emb_grad, emb_moment, emb_second, hot_rows, block_counts, dense_weight, dense_grad, dense_moment, dense_second):
    tables = lax.map(one_table, (emb_weight, emb_grad, emb_moment, emb_second, hot_rows, block_counts))
    summed_grad = lax.optimization_barrier(jnp.sum(dense_grad, axis=0))
    fresh_moment, fresh_second, heading = moments(dense_weight, summed_grad, dense_moment, dense_second)
    dense_scale = trust_step(jnp.sum(dense_weight * dense_weight), jnp.sum(heading * heading))
    fresh_dense = dense_weight - dense_scale * heading
    return (tables[0], tables[1], tables[2], tables[3], fresh_dense, fresh_moment, fresh_second)
```

```python
import functools

import jax
import jax.numpy as jnp
from jax import lax
from jax.experimental import pallas as pl
from jax.experimental.pallas import tpu as pltpu
from jax.sharding import PartitionSpec as P

BLOCK = 128


beta_one = 0.9
beta_two = 0.999
first_fix = 1.0 / (1.0 - 0.9**10)
second_fix = 1.0 / (1.0 - 0.999**10)
epsilon = 1e-06
norm_floor = 1e-06
decay_rate = 0.1
learn_rate = 0.05

MESH = pl.DeviceIdType.MESH
CORES = 2
PAIR = 2
WIRE = jnp.bfloat16


def moments(gradient, moment, second):
    new_moment = beta_one * moment + (1.0 - beta_one) * gradient
    new_second = beta_two * second + (1.0 - beta_two) * gradient * gradient
    direction = first_fix * new_moment / (jnp.sqrt(second_fix * new_second) + epsilon)
    return (new_moment, new_second, direction)


def trust_step(weight_sq, update_sq):
    return learn_rate * jnp.sqrt(weight_sq + norm_floor) / jnp.sqrt(update_sq + norm_floor)


def fold(x):
    return jnp.sum(x.reshape(-1, 8, x.shape[-1]), axis=0)


def full_sum(x):
    return jnp.sum(jnp.sum(x, axis=0, keepdims=True), axis=1, keepdims=True)


def exchange(
    n_rows, n_dp, chunks,
    rows_ref, count_ref, w_hbm, g_hbm, m_hbm, v_hbm, dg_hbm,
    s_ref, G_ref, hot_ref,
    w_buf, g_buf, m_buf, v_buf, u_buf, dg_buf,
    core_out, core_in, plane_out, plane_in, z_buf, sums, hot_w, hot_u,
    load_sem, dload_sem, core_sem, plane_send, plane_recv, up_sem, down_sem, z_recv,
    gather_send, gather_recv, twin_send, twin_recv,
    sum_send, sum_recv, hot_up, hot_down, hot_zrecv, hot_x, hot_xrecv,
):
    r, d = lax.axis_index("rows"), lax.axis_index("dp")
    core, y = lax.rem(r, CORES), lax.div(r, CORES)
    x, z = lax.rem(d, PAIR), lax.div(d, PAIR)
    ys, zs = n_rows // CORES, n_dp // PAIR
    quads = ys * PAIR
    q = y * PAIR + x
    twin = (y * CORES + 1 - core, d)
    side = (r, z * PAIR + 1 - x)
    above, below = (r, d + PAIR), (r, d - PAIR)
    has_above, has_below = z < zs - 1, z > 0

    def plane_peer(k):
        other = lax.rem(q + k, quads)
        oy, ox = lax.div(other, PAIR), lax.rem(other, PAIR)
        return other, (oy * CORES + core, z * PAIR + ox)

    def row_peer(k):
        other = lax.rem(r + k, n_rows)
        return other, (other, d)

    dload = pltpu.make_async_copy(dg_hbm.at[0], dg_buf, dload_sem)
    dload.start()
    span = w_buf.shape[0] // chunks

    def loads(c):
        here = pl.ds(pl.multiple_of(c * span, span), span)
        return [
            pltpu.make_async_copy(src.at[0, here], dst.at[here], load_sem.at[i, c])
            for i, (src, dst) in enumerate(
                ((w_hbm, w_buf), (g_hbm, g_buf), (m_hbm, m_buf), (v_hbm, v_buf))
            )
        ]

    for c in range(chunks):
        for copy in loads(c):
            copy.start()

    barrier = pltpu.get_barrier_semaphore()
    greeted = 0
    for k in range(1, n_rows):
        pl.semaphore_signal(barrier, inc=1, device_id=row_peer(k)[1], device_id_type=MESH)
        greeted += 1
    for oy in range(ys):
        pl.semaphore_signal(
            barrier, inc=1, device_id=(oy * CORES + core, z * PAIR + 1 - x), device_id_type=MESH
        )
        greeted += 1

    @pl.when(has_above)
    def _():
        pl.semaphore_signal(barrier, inc=1, device_id=above, device_id_type=MESH)

    @pl.when(has_below)
    def _():
        pl.semaphore_signal(barrier, inc=1, device_id=below, device_id_type=MESH)

    pl.semaphore_wait(
        barrier, greeted + has_above.astype(jnp.int32) + has_below.astype(jnp.int32)
    )

    half = dg_buf.shape[0] // CORES
    piece = half // quads
    dload.wait()
    theirs = pl.ds(pl.multiple_of((1 - core) * half, half), half)
    mine = pl.ds(pl.multiple_of(core * half, half), half)
    core_out[...] = dg_buf[theirs, :].astype(WIRE)
    core_copy = pltpu.make_async_remote_copy(
        src_ref=core_out, dst_ref=core_in, send_sem=core_sem.at[0], recv_sem=core_sem.at[1],
        device_id=twin, device_id_type=MESH,
    )
    core_copy.start()

    def step(c, carry):
        for copy in loads(c):
            copy.wait()
        wsq, usq = carry
        here = pl.ds(pl.multiple_of(c * span, span), span)
        w = w_buf[here, :]
        _, _, direction = moments(g_buf[here, :].astype(jnp.float32), m_buf[here, :], v_buf[here, :])
        u = direction + decay_rate * w
        u_buf[here, :] = u
        return wsq + fold(w * w), usq + fold(u * u)

    zero = jnp.zeros((8, w_buf.shape[1]), jnp.float32)
    wsq, usq = lax.fori_loop(0, chunks, step, (zero, zero))
    sums[r, 0] = wsq
    sums[r, 1] = usq

    def sum_copy(k, slot):
        return pltpu.make_async_remote_copy(
            src_ref=sums.at[slot], dst_ref=sums.at[slot],
            send_sem=sum_send.at[k], recv_sem=sum_recv.at[slot],
            device_id=row_peer(k)[1], device_id_type=MESH,
        )

    for k in range(1, n_rows):
        sum_copy(k, r).start()

    core_copy.wait()
    pair_sum = dg_buf[mine, :] + core_in[...].astype(jnp.float32)
    dg_buf[mine, :] = pair_sum
    plane_out[...] = pair_sum.astype(WIRE).reshape(plane_out.shape)

    def plane_copy(k, src_slot, dst_slot):
        return pltpu.make_async_remote_copy(
            src_ref=plane_out.at[src_slot], dst_ref=plane_in.at[dst_slot],
            send_sem=plane_send.at[k], recv_sem=plane_recv.at[dst_slot],
            device_id=plane_peer(k)[1], device_id_type=MESH,
        )

    for k in range(1, quads):
        plane_copy(k, plane_peer(k)[0], q).start()

    hot_n = hot_w.shape[0]

    def pick(j, carry):
        for i in range(8):
            at = rows_ref[0, 0, j * 8 + i]
            hot_w[pl.ds(j * 8 + i, 1), :] = w_buf[pl.ds(at, 1), :]
            hot_u[pl.ds(j * 8 + i, 1), :] = u_buf[pl.ds(at, 1), :]
        return carry

    lax.fori_loop(0, hot_n // 8, pick, 0)
    for k in range(1, n_rows):
        sum_copy(k, row_peer(k)[0]).wait_recv()
    total = jnp.sum(sums[...], axis=0)
    scale = trust_step(full_sum(total[0]), full_sum(total[1]))
    s_ref[...] = jnp.broadcast_to(scale, s_ref.shape)
    fresh = hot_w[...] - scale * hot_u[...]
    live = lax.broadcasted_iota(jnp.int32, fresh.shape, 0) < BLOCK * count_ref[0, 0]
    hot_ref[d, 0] = jnp.where(live, fresh, 0.0).astype(hot_ref.dtype)

    def hot_copy(block, send, recv, target):
        return pltpu.make_async_remote_copy(
            src_ref=hot_ref.at[block, 0], dst_ref=hot_ref.at[block, 0],
            send_sem=send, recv_sem=recv, device_id=target, device_id_type=MESH,
        )

    def hot_above(b):
        return hot_copy(b * PAIR + x, hot_up.at[b], hot_zrecv.at[b], above)

    def hot_below(b):
        return hot_copy(b * PAIR + x, hot_down.at[b], hot_zrecv.at[b], below)

    def hot_side(b):
        return hot_copy(b * PAIR + x, hot_x.at[b], hot_xrecv.at[b], side)

    def hot_from_side(b):
        return hot_copy(b * PAIR + 1 - x, hot_x.at[b], hot_xrecv.at[b], side)

    def z_copy(b, send, target):
        return pltpu.make_async_remote_copy(
            src_ref=z_buf.at[b], dst_ref=z_buf.at[b],
            send_sem=send.at[b], recv_sem=z_recv.at[b], device_id=target, device_id_type=MESH,
        )

    def relay(b, upward, downward, sidewards):
        if upward is not None:
            @pl.when(has_above)
            def _():
                upward(b).start()
        if downward is not None:
            @pl.when(has_below)
            def _():
                downward(b).start()
        if sidewards is not None:
            sidewards(b).start()

    z_above = lambda b: z_copy(b, up_sem, above)
    z_below = lambda b: z_copy(b, down_sem, below)
    relay(z, hot_above, hot_below, hot_side)

    for k in range(1, quads):
        plane_copy(k, 0, plane_peer(k)[0]).wait_recv()
    own = dg_buf[pl.ds(pl.multiple_of(core * half + q * piece, piece), piece), :]
    for k in range(1, quads):
        own = own + plane_in[plane_peer(k)[0]].astype(jnp.float32)
    z_buf[z] = own.astype(WIRE)
    relay(z, z_above, z_below, None)

    def both_ways(k, upward, downward, sidewards):
        low, high = z - k, z + k

        @pl.when(low >= 0)
        def _():
            upward(low).wait_recv()
            relay(low, upward, None, sidewards)

        @pl.when(high < zs)
        def _():
            downward(high).wait_recv()
            relay(high, None, downward, sidewards)

    for k in range(1, zs):
        both_ways(k, z_above, z_below, None)
        both_ways(k, hot_above, hot_below, hot_side)

    reduced = z_buf[0].astype(jnp.float32)
    for b in range(1, zs):
        reduced = reduced + z_buf[b].astype(jnp.float32)

    def slot(core_at, quad_at):
        return pl.ds(pl.multiple_of(core_at * half + quad_at * piece, piece), piece)

    G_ref[slot(core, q), :] = reduced.astype(WIRE)

    def gather_copy(k, quad_at):
        return pltpu.make_async_remote_copy(
            src_ref=G_ref.at[slot(core, quad_at)], dst_ref=G_ref.at[slot(core, quad_at)],
            send_sem=gather_send.at[k], recv_sem=gather_recv.at[quad_at],
            device_id=plane_peer(k)[1], device_id_type=MESH,
        )

    def twin_copy(core_at, quad_at):
        return pltpu.make_async_remote_copy(
            src_ref=G_ref.at[slot(core_at, quad_at)], dst_ref=G_ref.at[slot(core_at, quad_at)],
            send_sem=twin_send.at[quad_at], recv_sem=twin_recv.at[quad_at],
            device_id=twin, device_id_type=MESH,
        )

    for k in range(1, quads):
        gather_copy(k, q).start()
    twin_copy(core, q).start()
    for k in range(1, quads):
        other = plane_peer(k)[0]
        gather_copy(k, other).wait_recv()
        twin_copy(core, other).start()

    for b in range(zs):
        hot_from_side(b).wait_recv()
    for b in range(quads):
        twin_copy(1 - core, b).wait_recv()
    for b in range(quads):
        twin_copy(core, b).wait_send()
    for k in range(1, quads):
        gather_copy(k, q).wait_send()
        plane_copy(k, plane_peer(k)[0], q).wait_send()
    for k in range(1, n_rows):
        sum_copy(k, r).wait_send()
    for b in range(zs):
        hot_side(b).wait_send()

        @pl.when(jnp.logical_and(has_above, b <= z))
        def _():
            hot_above(b).wait_send()
            z_above(b).wait_send()

        @pl.when(jnp.logical_and(has_below, b >= z))
        def _():
            hot_below(b).wait_send()
            z_below(b).wait_send()


def shards(
    n_rows,
    n_dp,
    emb_weight,
    emb_grad,
    emb_moment,
    emb_second,
    hot_rows,
    block_counts,
    dense_weight,
    dense_grad,
    dense_moment,
    dense_second,
):
    _, rs, e = emb_weight.shape
    din, dout = dense_weight.shape
    hot_n = hot_rows.shape[2]
    quads, zs = n_rows // CORES * PAIR, n_dp // PAIR
    half = din // CORES
    piece = half // quads
    chunks = 6 if rs % (6 * 16) == 0 else 1
    f32 = jnp.float32
    dma = pltpu.SemaphoreType.DMA
    vmem = pl.BlockSpec(memory_space=pltpu.VMEM)
    smem = pl.BlockSpec(memory_space=pltpu.SMEM)
    hbm = pl.BlockSpec(memory_space=pl.ANY)
    step_size, summed_grad, hot_cache = pl.pallas_call(
        functools.partial(exchange, n_rows, n_dp, chunks),
        out_shape=(
            jax.ShapeDtypeStruct((8, e), f32),
            jax.ShapeDtypeStruct((din, dout), WIRE),
            jax.ShapeDtypeStruct((n_dp, 1, hot_n, e), jnp.bfloat16),
        ),
        in_specs=[smem, smem] + [hbm] * 5,
        out_specs=(vmem, vmem, vmem),
        scratch_shapes=[
            pltpu.VMEM((rs, e), f32),
            pltpu.VMEM((rs, e), emb_grad.dtype),
            pltpu.VMEM((rs, e), f32),
            pltpu.VMEM((rs, e), f32),
            pltpu.VMEM((rs, e), f32),
            pltpu.VMEM((din, dout), f32),
            pltpu.VMEM((half, dout), WIRE),
            pltpu.VMEM((half, dout), WIRE),
            pltpu.VMEM((quads, piece, dout), WIRE),
            pltpu.VMEM((quads, piece, dout), WIRE),
            pltpu.VMEM((zs, piece, dout), WIRE),
            pltpu.VMEM((n_rows, 2, 8, e), f32),
            pltpu.VMEM((hot_n, e), f32),
            pltpu.VMEM((hot_n, e), f32),
            dma((4, chunks)),
            dma,
            dma((2,)),
            dma((quads,)),
            dma((quads,)),
            dma((zs,)),
            dma((zs,)),
            dma((zs,)),
            dma((quads,)),
            dma((quads,)),
            dma((quads,)),
            dma((quads,)),
            dma((n_rows,)),
            dma((n_rows,)),
            dma((zs,)),
            dma((zs,)),
            dma((zs,)),
            dma((zs,)),
            dma((zs,)),
        ],
        compiler_params=pltpu.CompilerParams(
            collective_id=0, has_side_effects=True, vmem_limit_bytes=24 * 1024 * 1024
        ),
        name="exchange",
    )(hot_rows, block_counts, emb_weight, emb_grad, emb_moment, emb_second, dense_grad)

    new_moment, new_second, direction = moments(
        emb_grad.astype(f32), emb_moment, emb_second
    )
    update = direction + decay_rate * emb_weight
    new_weight = emb_weight - step_size[0, 0] * update
    fresh_moment, fresh_second, heading = moments(
        summed_grad.astype(f32), dense_moment, dense_second
    )
    dense_scale = trust_step(jnp.sum(dense_weight * dense_weight), jnp.sum(heading * heading))
    fresh_dense = dense_weight - dense_scale * heading
    return (new_weight, new_moment, new_second, hot_cache, fresh_dense, fresh_moment, fresh_second)


def solution(mesh):
    in_specs = (
        P("dp", "rows", None),
        P("dp", "rows", None),
        P("dp", "rows", None),
        P("dp", "rows", None),
        P("dp", "rows", None),
        P("dp", "rows"),
        P(),
        P(("rows", "dp"), None, None),
        P(),
        P(),
    )
    out_specs = (
        P("dp", "rows", None),
        P("dp", "rows", None),
        P("dp", "rows", None),
        P(None, "rows", None, None),
        P(),
        P(),
        P(),
    )
    body = functools.partial(shards, mesh.shape["rows"], mesh.shape["dp"])
    return jax.shard_map(body, mesh=mesh, in_specs=in_specs, out_specs=out_specs, check_vma=False)
```

```python
import functools

import jax
import jax.numpy as jnp
from jax import lax
from jax.experimental import pallas as pl
from jax.experimental.pallas import tpu as pltpu
from jax.sharding import PartitionSpec as P

BLOCK = 128


beta_one = 0.9
beta_two = 0.999
first_fix = 1.0 / (1.0 - 0.9**10)
second_fix = 1.0 / (1.0 - 0.999**10)
epsilon = 1e-06
norm_floor = 1e-06
decay_rate = 0.1
learn_rate = 0.05

MESH = pl.DeviceIdType.MESH
CORES = 2
PAIR = 2
WIRE = jnp.bfloat16
EXCHANGE_LIMIT = 40 * 1024 * 1024
WRITE_LIMIT = 1024 * 1024


def moments(gradient, moment, second):
    new_moment = beta_one * moment + (1.0 - beta_one) * gradient
    new_second = beta_two * second + (1.0 - beta_two) * gradient * gradient
    direction = first_fix * new_moment / (jnp.sqrt(second_fix * new_second) + epsilon)
    return (new_moment, new_second, direction)


def trust_step(weight_sq, update_sq):
    return learn_rate * jnp.sqrt(weight_sq + norm_floor) / jnp.sqrt(update_sq + norm_floor)


def fold(x):
    return jnp.sum(x.reshape(-1, 8, x.shape[-1]), axis=0)


def full_sum(x):
    return jnp.sum(jnp.sum(x, axis=0, keepdims=True), axis=1, keepdims=True)


def loop(start, stop, body):
    if stop - start <= 8:
        for i in range(start, stop):
            body(i)
    else:
        lax.fori_loop(start, stop, lambda i, carry: (body(i), carry)[1], 0)


def exchange(
    n_rows, n_dp, chunks, hot_first, hot_chunks, z_chunks,
    count_ref, rows_hbm, w_hbm, g_hbm, m_hbm, v_hbm, dg_hbm, dw_hbm, dm_hbm, dv_hbm,
    w_out, m_out, v_out, hot_ref, dw_out, dm_out, dv_out,
    rows_ref, w_buf, g_buf, m_buf, v_buf, u_buf, dg_buf, dw_buf, dm_buf, dv_buf, G_ref, U_buf,
    core_out, core_in, plane_out, plane_in, z_buf, sums, usqs, hot_w, hot_u,
    load_sem, dload_sem, core_send, core_recv, plane_send, plane_recv, up_sem, down_sem, z_recv,
    gather_send, gather_recv, twin_send, twin_recv,
    sum_send, sum_recv, hot_up, hot_down, hot_x, hot_recv,
):
    r, d = lax.axis_index("rows"), lax.axis_index("dp")
    core, y = lax.rem(r, CORES), lax.div(r, CORES)
    x, z = lax.rem(d, PAIR), lax.div(d, PAIR)
    ys, zs = n_rows // CORES, n_dp // PAIR
    quads = ys * PAIR
    q = y * PAIR + x
    twin = (y * CORES + 1 - core, d)
    side = (r, z * PAIR + 1 - x)
    above, below = (r, d + PAIR), (r, d - PAIR)
    has_above, has_below = z < zs - 1, z > 0

    def plane_peer(k):
        other = lax.rem(q + k, quads)
        oy, ox = lax.div(other, PAIR), lax.rem(other, PAIR)
        return other, (oy * CORES + core, z * PAIR + ox)

    def row_peer(k):
        other = lax.rem(r + k, n_rows)
        return other, (other, d)

    dloads = [
        pltpu.make_async_copy(src, dst, dload_sem.at[i])
        for i, (src, dst) in enumerate(
            (
                (dg_hbm.at[0], dg_buf), (dw_hbm, dw_buf), (dm_hbm, dm_buf), (dv_hbm, dv_buf),
                (rows_hbm, rows_ref),
            )
        )
    ]
    dloads[0].start()
    span = w_buf.shape[0] // chunks

    def loads(c):
        here = pl.ds(pl.multiple_of(c * span, span), span)
        return [
            pltpu.make_async_copy(src.at[0, here], dst.at[here], load_sem.at[i, c])
            for i, (src, dst) in enumerate(
                ((w_hbm, w_buf), (g_hbm, g_buf), (m_hbm, m_buf), (v_hbm, v_buf))
            )
        ]

    for c in range(chunks):
        for copy in loads(c):
            copy.start()
    for copy in dloads[1:]:
        copy.start()

    barrier = pltpu.get_barrier_semaphore()
    greeted = 0
    for k in range(1, n_rows):
        pl.semaphore_signal(barrier, inc=1, device_id=row_peer(k)[1], device_id_type=MESH)
        greeted += 1
    for oy in range(ys):
        pl.semaphore_signal(
            barrier, inc=1, device_id=(oy * CORES + core, z * PAIR + 1 - x), device_id_type=MESH
        )
        greeted += 1

    @pl.when(has_above)
    def _():
        pl.semaphore_signal(barrier, inc=1, device_id=above, device_id_type=MESH)

    @pl.when(has_below)
    def _():
        pl.semaphore_signal(barrier, inc=1, device_id=below, device_id_type=MESH)

    pl.semaphore_wait(
        barrier, greeted + has_above.astype(jnp.int32) + has_below.astype(jnp.int32)
    )

    half = dg_buf.shape[0] // CORES
    piece = half // quads

    def slot(core_at, quad_at):
        return pl.ds(pl.multiple_of(core_at * half + quad_at * piece, piece), piece)

    def core_copy(quad_at):
        return pltpu.make_async_remote_copy(
            src_ref=core_out.at[quad_at], dst_ref=core_in.at[quad_at],
            send_sem=core_send.at[quad_at], recv_sem=core_recv.at[quad_at],
            device_id=twin, device_id_type=MESH,
        )

    dloads[0].wait()
    for k in range(1, quads + 1):
        other = lax.rem(q + k, quads)
        core_out[other] = dg_buf[slot(1 - core, other), :].astype(WIRE)
        core_copy(other).start()

    def step(c, carry):
        for copy in loads(c):
            copy.wait()
        wsq, usq = carry
        here = pl.ds(pl.multiple_of(c * span, span), span)
        w = w_buf[here, :]
        m, v, direction = moments(g_buf[here, :].astype(jnp.float32), m_buf[here, :], v_buf[here, :])
        u = direction + decay_rate * w
        u_buf[here, :] = u
        m_out[0, here, :] = m
        v_out[0, here, :] = v
        return wsq + fold(w * w), usq + fold(u * u)

    def plane_copy(k, src_slot, dst_slot):
        return pltpu.make_async_remote_copy(
            src_ref=plane_out.at[src_slot], dst_ref=plane_in.at[dst_slot],
            send_sem=plane_send.at[k], recv_sem=plane_recv.at[dst_slot],
            device_id=plane_peer(k)[1], device_id_type=MESH,
        )

    zero = jnp.zeros((8, w_buf.shape[1]), jnp.float32)
    early = chunks // 2
    partial = lax.fori_loop(0, early, step, (zero, zero))

    for k in range(1, quads):
        other = plane_peer(k)[0]
        core_copy(other).wait_recv()
        plane_out[other] = (
            dg_buf[slot(core, other), :] + core_in[other].astype(jnp.float32)
        ).astype(WIRE)
        plane_copy(k, other, q).start()

    wsq, usq = lax.fori_loop(early, chunks, step, partial)
    sums[r, 0] = wsq
    sums[r, 1] = usq

    def sum_copy(k, slot):
        return pltpu.make_async_remote_copy(
            src_ref=sums.at[slot], dst_ref=sums.at[slot],
            send_sem=sum_send.at[k], recv_sem=sum_recv.at[slot],
            device_id=row_peer(k)[1], device_id_type=MESH,
        )

    for k in range(1, n_rows):
        sum_copy(k, r).start()

    core_copy(q).wait_recv()
    own = dg_buf[slot(core, q), :] + core_in[q].astype(jnp.float32)
    for k in range(1, quads):
        other = plane_peer(k)[0]
        plane_copy(k, 0, other).wait_recv()
        own = own + plane_in[other].astype(jnp.float32)
    z_buf[z] = own.astype(WIRE).reshape(z_buf.shape[1:])

    def z_copy(b, c, send, target):
        return pltpu.make_async_remote_copy(
            src_ref=z_buf.at[b, c], dst_ref=z_buf.at[b, c],
            send_sem=send.at[b, c], recv_sem=z_recv.at[b, c], device_id=target, device_id_type=MESH,
        )

    hot_rows_at = hot_ref.shape[2] // hot_chunks

    def hot_copy(block, c, send, target):
        here = pl.ds(c * hot_rows_at, hot_rows_at)
        return pltpu.make_async_remote_copy(
            src_ref=hot_ref.at[block, 0, here], dst_ref=hot_ref.at[block, 0, here],
            send_sem=send.at[block, c], recv_sem=hot_recv.at[block, c],
            device_id=target, device_id_type=MESH,
        )

    def on(condition, action):
        @pl.when(condition)
        def _():
            action()

    def z_all(b, up, down):
        for c in range(z_chunks):
            if up:
                z_copy(b, c, up_sem, above).start()
            if down:
                z_copy(b, c, down_sem, below).start()

    on(has_above, lambda: z_all(z, True, False))
    on(has_below, lambda: z_all(z, False, True))

    hot_n = hot_w.shape[0]

    def pick(j, carry):
        for i in range(8):
            at = rows_ref[0, 0, j * 8 + i]
            hot_w[pl.ds(j * 8 + i, 1), :] = w_buf[pl.ds(at, 1), :]
            hot_u[pl.ds(j * 8 + i, 1), :] = u_buf[pl.ds(at, 1), :]
        return carry

    for copy in dloads[4:]:
        copy.wait()
    lax.fori_loop(0, hot_n // 8, pick, 0)
    for k in range(1, n_rows):
        sum_copy(k, row_peer(k)[0]).wait_recv()
    total = jnp.sum(sums[...], axis=0)
    scale = trust_step(full_sum(total[0]), full_sum(total[1]))
    fresh = hot_w[...] - scale * hot_u[...]
    live = lax.broadcasted_iota(jnp.int32, fresh.shape, 0) < BLOCK * count_ref[0, 0]
    hot_ref[d, 0] = jnp.where(live, fresh, 0.0).astype(hot_ref.dtype)

    order = list(range(hot_first, hot_chunks)) + list(range(hot_first))
    for c in order:
        hot_copy(d, c, hot_x, side).start()
        on(has_above, lambda: hot_copy(d, c, hot_up, above).start())
        on(has_below, lambda: hot_copy(d, c, hot_down, below).start())

    def renew(c, carry):
        here = pl.ds(pl.multiple_of(c * span, span), span)
        w_out[0, here, :] = w_buf[here, :] - scale * u_buf[here, :]
        return carry

    lax.fori_loop(0, chunks, renew, 0)

    across = z * PAIR + 1 - x
    for c in range(hot_first, hot_chunks):
        hot_copy(across, c, hot_x, side).wait_recv()
        on(has_above, lambda: hot_copy(across, c, hot_up, above).start())
        on(has_below, lambda: hot_copy(across, c, hot_down, below).start())

    def both_ways(k):
        low, high = z - k, z + k

        def dense_from(b, send, target, onward):
            def run():
                for c in range(z_chunks):
                    z_copy(b, c, send, target).wait_recv()
                    on(onward, lambda: z_copy(b, c, send, target).start())
            return run

        on(low >= 0, dense_from(low, up_sem, above, has_above))
        on(high < zs, dense_from(high, down_sem, below, has_below))

        def hot_from(b, c, column, send, target, onward, sidewards):
            def run():
                block = b * PAIR + column
                hot_copy(block, c, send, target).wait_recv()
                on(onward, lambda: hot_copy(block, c, send, target).start())
                if sidewards:
                    hot_copy(block, c, hot_x, side).start()
            return run

        for c in order:
            columns = (x,) if c < hot_first else (x, 1 - x)
            for column in columns:
                on(low >= 0, hot_from(low, c, column, hot_up, above, has_above, c < hot_first))
                on(high < zs, hot_from(high, c, column, hot_down, below, has_below, c < hot_first))

    loop(1, zs, both_ways)

    reduced = z_buf[0].astype(jnp.float32)
    for b in range(1, zs):
        reduced = reduced + z_buf[b].astype(jnp.float32)
    G_ref[slot(core, q), :] = reduced.astype(WIRE).reshape(piece, -1)

    def gather_copy(k, quad_at):
        return pltpu.make_async_remote_copy(
            src_ref=G_ref.at[slot(core, quad_at)], dst_ref=G_ref.at[slot(core, quad_at)],
            send_sem=gather_send.at[k], recv_sem=gather_recv.at[quad_at],
            device_id=plane_peer(k)[1], device_id_type=MESH,
        )

    def twin_copy(core_at, quad_at):
        return pltpu.make_async_remote_copy(
            src_ref=G_ref.at[slot(core_at, quad_at)], dst_ref=G_ref.at[slot(core_at, quad_at)],
            send_sem=twin_send.at[quad_at], recv_sem=twin_recv.at[quad_at],
            device_id=twin, device_id_type=MESH,
        )

    for k in range(1, quads):
        gather_copy(k, q).start()
    twin_copy(core, q).start()

    for copy in dloads[1:4]:
        copy.wait()

    def dense_piece(core_at, quad_at):
        here = slot(core_at, quad_at)
        m, v, heading = moments(G_ref[here, :].astype(jnp.float32), dm_buf[here, :], dv_buf[here, :])
        dm_out[here, :] = m
        dv_out[here, :] = v
        U_buf[here, :] = heading
        usqs[core_at * quads + quad_at] = fold(heading * heading)

    weight_sq = full_sum(fold(dw_buf[...] * dw_buf[...]))
    dense_piece(core, q)
    for k in range(1, quads):
        other = plane_peer(k)[0]
        gather_copy(k, other).wait_recv()
        twin_copy(core, other).start()
        dense_piece(core, other)
    for k in range(quads):
        other = lax.rem(q + k, quads)
        twin_copy(1 - core, other).wait_recv()
        dense_piece(1 - core, other)
    dense_scale = trust_step(weight_sq, full_sum(jnp.sum(usqs[...], axis=0)))
    dw_out[...] = dw_buf[...] - dense_scale * U_buf[...]

    def hot_wait_side(b):
        for c in range(hot_first):
            hot_copy(b * PAIR + 1 - x, c, hot_x, side).wait_recv()
            hot_copy(b * PAIR + x, c, hot_x, side).wait_send()

    loop(0, zs, hot_wait_side)
    for c in range(hot_first, hot_chunks):
        hot_copy(d, c, hot_x, side).wait_send()
    for k in range(quads):
        core_copy(k).wait_send()
        twin_copy(core, k).wait_send()
    for k in range(1, quads):
        gather_copy(k, q).wait_send()
        plane_copy(k, 0, q).wait_send()
    for k in range(1, n_rows):
        sum_copy(k, r).wait_send()

    def sent(b):
        def run(z_sem, hot_sem, target):
            def go():
                for c in range(z_chunks):
                    z_copy(b, c, z_sem, target).wait_send()
                for c in range(hot_chunks):
                    hot_copy(b * PAIR + x, c, hot_sem, target).wait_send()
                    if c >= hot_first:
                        hot_copy(b * PAIR + 1 - x, c, hot_sem, target).wait_send()
            return go

        on(jnp.logical_and(has_above, b <= z), run(up_sem, hot_up, above))
        on(jnp.logical_and(has_below, b >= z), run(down_sem, hot_down, below))

    loop(0, zs, sent)


def write_out(n, *refs):
    sources, targets, sem = refs[:n], refs[n:2 * n], refs[2 * n]
    copies = [
        pltpu.make_async_copy(src, dst, sem.at[i])
        for i, (src, dst) in enumerate(zip(sources, targets))
    ]
    for copy in copies:
        copy.start()
    for copy in copies:
        copy.wait()


def shards(
    n_rows,
    n_dp,
    emb_weight,
    emb_grad,
    emb_moment,
    emb_second,
    hot_rows,
    block_counts,
    dense_weight,
    dense_grad,
    dense_moment,
    dense_second,
):
    _, rs, e = emb_weight.shape
    din, dout = dense_weight.shape
    hot_n = hot_rows.shape[2]
    quads, zs = n_rows // CORES * PAIR, n_dp // PAIR
    half = din // CORES
    piece = half // quads
    chunks = 6 if rs % (6 * 16) == 0 else 1
    hot_first, hot_chunks = 2, 4
    z_chunks = 2
    f32 = jnp.float32
    dma = pltpu.SemaphoreType.DMA
    vmem = pl.BlockSpec(memory_space=pltpu.VMEM)
    hbm = pl.BlockSpec(memory_space=pltpu.HBM)
    shapes = (
        jax.ShapeDtypeStruct((1, rs, e), f32),
        jax.ShapeDtypeStruct((1, rs, e), f32),
        jax.ShapeDtypeStruct((1, rs, e), f32),
        jax.ShapeDtypeStruct((n_dp, 1, hot_n, e), jnp.bfloat16),
        jax.ShapeDtypeStruct((din, dout), f32),
        jax.ShapeDtypeStruct((din, dout), f32),
        jax.ShapeDtypeStruct((din, dout), f32),
    )
    outs = pl.pallas_call(
        functools.partial(exchange, n_rows, n_dp, chunks, hot_first, hot_chunks, z_chunks),
        out_shape=tuple(pltpu.VMEM(shape.shape, shape.dtype) for shape in shapes),
        in_specs=[pl.BlockSpec(memory_space=pltpu.SMEM)] + [hbm] * 9,
        out_specs=(vmem,) * 7,
        scratch_shapes=[
            pltpu.SMEM(hot_rows.shape, jnp.int32),
            pltpu.VMEM((rs, e), f32),
            pltpu.VMEM((rs, e), emb_grad.dtype),
            pltpu.VMEM((rs, e), f32),
            pltpu.VMEM((rs, e), f32),
            pltpu.VMEM((rs, e), f32),
            pltpu.VMEM((din, dout), f32),
            pltpu.VMEM((din, dout), f32),
            pltpu.VMEM((din, dout), f32),
            pltpu.VMEM((din, dout), f32),
            pltpu.VMEM((din, dout), WIRE),
            pltpu.VMEM((din, dout), f32),
            pltpu.VMEM((quads, piece, dout), WIRE),
            pltpu.VMEM((quads, piece, dout), WIRE),
            pltpu.VMEM((quads, piece, dout), WIRE),
            pltpu.VMEM((quads, piece, dout), WIRE),
            pltpu.VMEM((zs, z_chunks, piece // z_chunks, dout), WIRE),
            pltpu.VMEM((n_rows, 2, 8, e), f32),
            pltpu.VMEM((CORES * quads, 8, dout), f32),
            pltpu.VMEM((hot_n, e), f32),
            pltpu.VMEM((hot_n, e), f32),
            dma((4, chunks)),
            dma((5,)),
            dma((quads,)),
            dma((quads,)),
            dma((quads,)),
            dma((quads,)),
            dma((zs, z_chunks)),
            dma((zs, z_chunks)),
            dma((zs, z_chunks)),
            dma((quads,)),
            dma((quads,)),
            dma((quads,)),
            dma((quads,)),
            dma((n_rows,)),
            dma((n_rows,)),
            dma((n_dp, hot_chunks)),
            dma((n_dp, hot_chunks)),
            dma((n_dp, hot_chunks)),
            dma((n_dp, hot_chunks)),
        ],
        compiler_params=pltpu.CompilerParams(
            collective_id=0, has_side_effects=True, vmem_limit_bytes=EXCHANGE_LIMIT
        ),
        name="exchange",
    )(
        block_counts,
        *(
            pltpu.with_memory_space_constraint(a, pltpu.HBM)
            for a in (
                hot_rows, emb_weight, emb_grad, emb_moment, emb_second,
                dense_grad, dense_weight, dense_moment, dense_second,
            )
        ),
    )
    return pl.pallas_call(
        functools.partial(write_out, len(shapes)),
        out_shape=shapes,
        in_specs=[vmem] * len(shapes),
        out_specs=(hbm,) * len(shapes),
        scratch_shapes=[dma((len(shapes),))],
        compiler_params=pltpu.CompilerParams(vmem_limit_bytes=WRITE_LIMIT),
        name="write_out",
    )(*outs)


def solution(mesh):
    in_specs = (
        P("dp", "rows", None),
        P("dp", "rows", None),
        P("dp", "rows", None),
        P("dp", "rows", None),
        P("dp", "rows", None),
        P("dp", "rows"),
        P(),
        P(("rows", "dp"), None, None),
        P(),
        P(),
    )
    out_specs = (
        P("dp", "rows", None),
        P("dp", "rows", None),
        P("dp", "rows", None),
        P(None, "rows", None, None),
        P(),
        P(),
        P(),
    )
    body = functools.partial(shards, mesh.shape["rows"], mesh.shape["dp"])
    return jax.shard_map(body, mesh=mesh, in_specs=in_specs, out_specs=out_specs, check_vma=False)
```

```python
import functools

import jax
import jax.numpy as jnp
from jax import lax
from jax.experimental import pallas as pl
from jax.experimental.pallas import tpu as pltpu
from jax.sharding import PartitionSpec as P

BLOCK = 128


beta_one = 0.9
beta_two = 0.999
first_fix = 1.0 / (1.0 - 0.9**10)
second_fix = 1.0 / (1.0 - 0.999**10)
epsilon = 1e-06
norm_floor = 1e-06
decay_rate = 0.1
learn_rate = 0.05

MESH = pl.DeviceIdType.MESH
CORES = 2
PAIR = 2
WIRE = jnp.bfloat16
LATE = 1
EXCHANGE_LIMIT = 40 * 1024 * 1024
WRITE_LIMIT = 1024 * 1024


def moments(gradient, moment, second):
    new_moment = beta_one * moment + (1.0 - beta_one) * gradient
    new_second = beta_two * second + (1.0 - beta_two) * gradient * gradient
    direction = first_fix * new_moment / (jnp.sqrt(second_fix * new_second) + epsilon)
    return (new_moment, new_second, direction)


def trust_step(weight_sq, update_sq):
    return learn_rate * jnp.sqrt(weight_sq + norm_floor) / jnp.sqrt(update_sq + norm_floor)


def fold(x):
    return jnp.sum(x.reshape(-1, 8, x.shape[-1]), axis=0)


def full_sum(x):
    return jnp.sum(jnp.sum(x, axis=0, keepdims=True), axis=1, keepdims=True)


def loop(start, stop, body):
    if stop - start <= 8:
        for i in range(start, stop):
            body(i)
    else:
        lax.fori_loop(start, stop, lambda i, carry: (body(i), carry)[1], 0)


def exchange(
    n_rows, n_dp, chunks, hot_first, hot_chunks,
    count_ref, rows_hbm, w_hbm, g_hbm, m_hbm, v_hbm, dg_hbm, dw_hbm, dm_hbm, dv_hbm,
    w_out, m_out, v_out, hot_ref, dw_out, dm_out, dv_out,
    rows_ref, w_buf, g_buf, m_buf, v_buf, u_buf, dg_buf, dw_buf, dm_buf, dv_buf, G_ref, U_buf,
    core_out, core_in, plane_out, plane_in, z_buf, sums, usqs, hot_w, hot_u,
    load_sem, dload_sem, core_send, core_recv, plane_send, plane_recv, z_send, z_recv,
    gather_send, gather_recv, twin_send, twin_recv,
    sum_send, sum_recv, hot_up, hot_down, hot_x, hot_recv,
):
    r, d = lax.axis_index("rows"), lax.axis_index("dp")
    core, y = lax.rem(r, CORES), lax.div(r, CORES)
    x, z = lax.rem(d, PAIR), lax.div(d, PAIR)
    ys, zs = n_rows // CORES, n_dp // PAIR
    quads = ys * PAIR
    q = y * PAIR + x
    twin = (y * CORES + 1 - core, d)
    side = (r, z * PAIR + 1 - x)
    above, below = (r, d + PAIR), (r, d - PAIR)
    has_above, has_below = z < zs - 1, z > 0

    def plane_peer(k):
        other = lax.rem(q + k, quads)
        oy, ox = lax.div(other, PAIR), lax.rem(other, PAIR)
        return other, (oy * CORES + core, z * PAIR + ox)

    def line_peer(k):
        other = lax.rem(z + k, zs)
        return other, (r, other * PAIR + x)

    def row_peer(k):
        other = lax.rem(r + k, n_rows)
        return other, (other, d)

    dloads = [
        pltpu.make_async_copy(src, dst, dload_sem.at[i])
        for i, (src, dst) in enumerate(
            (
                (dg_hbm.at[0], dg_buf), (dw_hbm, dw_buf), (dm_hbm, dm_buf), (dv_hbm, dv_buf),
                (rows_hbm, rows_ref),
            )
        )
    ]
    dloads[0].start()
    span = w_buf.shape[0] // chunks

    def loads(c):
        here = pl.ds(pl.multiple_of(c * span, span), span)
        return [
            pltpu.make_async_copy(src.at[0, here], dst.at[here], load_sem.at[i, c])
            for i, (src, dst) in enumerate(
                ((w_hbm, w_buf), (g_hbm, g_buf), (m_hbm, m_buf), (v_hbm, v_buf))
            )
        ]

    for c in range(chunks):
        for copy in loads(c):
            copy.start()
    for copy in dloads[1:]:
        copy.start()

    barrier = pltpu.get_barrier_semaphore()
    greeted = 0
    for k in range(1, n_rows):
        pl.semaphore_signal(barrier, inc=1, device_id=row_peer(k)[1], device_id_type=MESH)
        greeted += 1
    for oy in range(ys):
        pl.semaphore_signal(
            barrier, inc=1, device_id=(oy * CORES + core, z * PAIR + 1 - x), device_id_type=MESH
        )
        greeted += 1

    for k in range(1, zs):
        pl.semaphore_signal(barrier, inc=1, device_id=line_peer(k)[1], device_id_type=MESH)
        greeted += 1
    pl.semaphore_wait(barrier, greeted)

    half = dg_buf.shape[0] // CORES
    piece = half // quads

    def slot(core_at, quad_at):
        return pl.ds(pl.multiple_of(core_at * half + quad_at * piece, piece), piece)

    def core_copy(quad_at):
        return pltpu.make_async_remote_copy(
            src_ref=core_out.at[quad_at], dst_ref=core_in.at[quad_at],
            send_sem=core_send.at[quad_at], recv_sem=core_recv.at[quad_at],
            device_id=twin, device_id_type=MESH,
        )

    dloads[0].wait()
    for k in range(1, quads + 1):
        other = lax.rem(q + k, quads)
        core_out[other] = dg_buf[slot(1 - core, other), :].astype(WIRE)
        core_copy(other).start()

    def step(c, carry):
        for copy in loads(c):
            copy.wait()
        wsq, usq = carry
        here = pl.ds(pl.multiple_of(c * span, span), span)
        w = w_buf[here, :]
        m, v, direction = moments(g_buf[here, :].astype(jnp.float32), m_buf[here, :], v_buf[here, :])
        u = direction + decay_rate * w
        u_buf[here, :] = u
        m_out[0, here, :] = m
        v_out[0, here, :] = v
        return wsq + fold(w * w), usq + fold(u * u)

    def plane_copy(k, src_slot, dst_slot):
        return pltpu.make_async_remote_copy(
            src_ref=plane_out.at[src_slot], dst_ref=plane_in.at[dst_slot],
            send_sem=plane_send.at[k], recv_sem=plane_recv.at[dst_slot],
            device_id=plane_peer(k)[1], device_id_type=MESH,
        )

    zero = jnp.zeros((8, w_buf.shape[1]), jnp.float32)
    early = chunks // 2
    partial = lax.fori_loop(0, early, step, (zero, zero))

    for k in range(1, quads):
        other = plane_peer(k)[0]
        core_copy(other).wait_recv()
        plane_out[other] = (
            dg_buf[slot(core, other), :] + core_in[other].astype(jnp.float32)
        ).astype(WIRE)
        plane_copy(k, other, q).start()

    wsq, usq = lax.fori_loop(early, chunks, step, partial)
    sums[r, 0] = wsq
    sums[r, 1] = usq

    def sum_copy(k, slot):
        return pltpu.make_async_remote_copy(
            src_ref=sums.at[slot], dst_ref=sums.at[slot],
            send_sem=sum_send.at[k], recv_sem=sum_recv.at[slot],
            device_id=row_peer(k)[1], device_id_type=MESH,
        )

    for k in range(1, n_rows):
        sum_copy(k, r).start()

    hot_rows_at = hot_ref.shape[2] // hot_chunks

    def hot_copy(block, c, send, target):
        here = pl.ds(c * hot_rows_at, hot_rows_at)
        return pltpu.make_async_remote_copy(
            src_ref=hot_ref.at[block, 0, here], dst_ref=hot_ref.at[block, 0, here],
            send_sem=send.at[block, c], recv_sem=hot_recv.at[block, c],
            device_id=target, device_id_type=MESH,
        )

    def on(condition, action):
        @pl.when(condition)
        def _():
            action()

    hot_n = hot_w.shape[0]

    def pick(j, carry):
        for i in range(8):
            at = rows_ref[0, 0, j * 8 + i]
            hot_w[pl.ds(j * 8 + i, 1), :] = w_buf[pl.ds(at, 1), :]
            hot_u[pl.ds(j * 8 + i, 1), :] = u_buf[pl.ds(at, 1), :]
        return carry

    for copy in dloads[4:]:
        copy.wait()
    lax.fori_loop(0, hot_n // 8, pick, 0)
    for k in range(1, n_rows):
        sum_copy(k, row_peer(k)[0]).wait_recv()
    total = jnp.sum(sums[...], axis=0)
    scale = trust_step(full_sum(total[0]), full_sum(total[1]))
    fresh = hot_w[...] - scale * hot_u[...]
    live = lax.broadcasted_iota(jnp.int32, fresh.shape, 0) < BLOCK * count_ref[0, 0]
    hot_ref[d, 0] = jnp.where(live, fresh, 0.0).astype(hot_ref.dtype)

    order = list(range(hot_first, hot_chunks)) + list(range(hot_first))
    for c in order:
        hot_copy(d, c, hot_x, side).start()
        on(has_above, lambda: hot_copy(d, c, hot_up, above).start())
        on(has_below, lambda: hot_copy(d, c, hot_down, below).start())

    core_copy(q).wait_recv()
    own = dg_buf[slot(core, q), :] + core_in[q].astype(jnp.float32)
    for k in range(1, quads):
        other = plane_peer(k)[0]
        plane_copy(k, 0, other).wait_recv()
        own = own + plane_in[other].astype(jnp.float32)
    z_buf[z] = own.astype(WIRE)

    def z_copy(k, slot_at):
        return pltpu.make_async_remote_copy(
            src_ref=z_buf.at[slot_at], dst_ref=z_buf.at[slot_at],
            send_sem=z_send.at[k], recv_sem=z_recv.at[slot_at],
            device_id=line_peer(k)[1], device_id_type=MESH,
        )

    for k in range(1, zs):
        z_copy(k, z).start()

    def renew(c, carry):
        here = pl.ds(pl.multiple_of(c * span, span), span)
        w_out[0, here, :] = w_buf[here, :] - scale * u_buf[here, :]
        return carry

    lax.fori_loop(0, chunks, renew, 0)

    across = z * PAIR + 1 - x
    for c in range(hot_first, hot_chunks):
        hot_copy(across, c, hot_x, side).wait_recv()
        on(has_above, lambda: hot_copy(across, c, hot_up, above).start())
        on(has_below, lambda: hot_copy(across, c, hot_down, below).start())

    def both_ways(k):
        low, high = z - k, z + k

        def hot_from(b, c, column, send, target, onward, sidewards):
            def run():
                block = b * PAIR + column
                hot_copy(block, c, send, target).wait_recv()
                on(onward, lambda: hot_copy(block, c, send, target).start())
                if sidewards:
                    hot_copy(block, c, hot_x, side).start()
            return run

        for c in order:
            columns = (x,) if c < hot_first else (x, 1 - x)
            for column in columns:
                on(low >= 0, hot_from(low, c, column, hot_up, above, has_above, c < hot_first))
                on(high < zs, hot_from(high, c, column, hot_down, below, has_below, c < hot_first))

    last = max(1, zs - LATE)
    loop(1, last, both_ways)

    for k in range(1, zs):
        z_copy(k, line_peer(k)[0]).wait_recv()
    reduced = z_buf[0].astype(jnp.float32)
    for b in range(1, zs):
        reduced = reduced + z_buf[b].astype(jnp.float32)
    G_ref[slot(core, q), :] = reduced.astype(WIRE)

    def gather_copy(k, quad_at):
        return pltpu.make_async_remote_copy(
            src_ref=G_ref.at[slot(core, quad_at)], dst_ref=G_ref.at[slot(core, quad_at)],
            send_sem=gather_send.at[k], recv_sem=gather_recv.at[quad_at],
            device_id=plane_peer(k)[1], device_id_type=MESH,
        )

    def twin_copy(core_at, quad_at):
        return pltpu.make_async_remote_copy(
            src_ref=G_ref.at[slot(core_at, quad_at)], dst_ref=G_ref.at[slot(core_at, quad_at)],
            send_sem=twin_send.at[quad_at], recv_sem=twin_recv.at[quad_at],
            device_id=twin, device_id_type=MESH,
        )

    for k in range(1, quads):
        gather_copy(k, q).start()
    twin_copy(core, q).start()

    loop(last, zs, both_ways)

    for copy in dloads[1:4]:
        copy.wait()

    def dense_piece(core_at, quad_at):
        here = slot(core_at, quad_at)
        m, v, heading = moments(G_ref[here, :].astype(jnp.float32), dm_buf[here, :], dv_buf[here, :])
        dm_out[here, :] = m
        dv_out[here, :] = v
        U_buf[here, :] = heading
        usqs[core_at * quads + quad_at] = fold(heading * heading)

    weight_sq = full_sum(fold(dw_buf[...] * dw_buf[...]))
    dense_piece(core, q)
    for k in range(1, quads):
        other = plane_peer(k)[0]
        gather_copy(k, other).wait_recv()
        twin_copy(core, other).start()
        dense_piece(core, other)
    for k in range(quads):
        other = lax.rem(q + k, quads)
        twin_copy(1 - core, other).wait_recv()
        dense_piece(1 - core, other)
    dense_scale = trust_step(weight_sq, full_sum(jnp.sum(usqs[...], axis=0)))
    dw_out[...] = dw_buf[...] - dense_scale * U_buf[...]

    def hot_wait_side(b):
        for c in range(hot_first):
            hot_copy(b * PAIR + 1 - x, c, hot_x, side).wait_recv()
            hot_copy(b * PAIR + x, c, hot_x, side).wait_send()

    loop(0, zs, hot_wait_side)
    for c in range(hot_first, hot_chunks):
        hot_copy(d, c, hot_x, side).wait_send()
    for k in range(quads):
        core_copy(k).wait_send()
        twin_copy(core, k).wait_send()
    for k in range(1, quads):
        gather_copy(k, q).wait_send()
        plane_copy(k, 0, q).wait_send()
    for k in range(1, n_rows):
        sum_copy(k, r).wait_send()
    for k in range(1, zs):
        z_copy(k, z).wait_send()

    def sent(b):
        def run(hot_sem, target):
            def go():
                for c in range(hot_chunks):
                    hot_copy(b * PAIR + x, c, hot_sem, target).wait_send()
                    if c >= hot_first:
                        hot_copy(b * PAIR + 1 - x, c, hot_sem, target).wait_send()
            return go

        on(jnp.logical_and(has_above, b <= z), run(hot_up, above))
        on(jnp.logical_and(has_below, b >= z), run(hot_down, below))

    loop(0, zs, sent)


def write_out(n, *refs):
    sources, targets, sem = refs[:n], refs[n:2 * n], refs[2 * n]
    copies = [
        pltpu.make_async_copy(src, dst, sem.at[i])
        for i, (src, dst) in enumerate(zip(sources, targets))
    ]
    for copy in copies:
        copy.start()
    for copy in copies:
        copy.wait()


def shards(
    n_rows,
    n_dp,
    emb_weight,
    emb_grad,
    emb_moment,
    emb_second,
    hot_rows,
    block_counts,
    dense_weight,
    dense_grad,
    dense_moment,
    dense_second,
):
    _, rs, e = emb_weight.shape
    din, dout = dense_weight.shape
    hot_n = hot_rows.shape[2]
    quads, zs = n_rows // CORES * PAIR, n_dp // PAIR
    half = din // CORES
    piece = half // quads
    chunks = 6 if rs % (6 * 16) == 0 else 1
    hot_first, hot_chunks = 4, 4
    f32 = jnp.float32
    dma = pltpu.SemaphoreType.DMA
    vmem = pl.BlockSpec(memory_space=pltpu.VMEM)
    hbm = pl.BlockSpec(memory_space=pltpu.HBM)
    shapes = (
        jax.ShapeDtypeStruct((1, rs, e), f32),
        jax.ShapeDtypeStruct((1, rs, e), f32),
        jax.ShapeDtypeStruct((1, rs, e), f32),
        jax.ShapeDtypeStruct((n_dp, 1, hot_n, e), jnp.bfloat16),
        jax.ShapeDtypeStruct((din, dout), f32),
        jax.ShapeDtypeStruct((din, dout), f32),
        jax.ShapeDtypeStruct((din, dout), f32),
    )
    outs = pl.pallas_call(
        functools.partial(exchange, n_rows, n_dp, chunks, hot_first, hot_chunks),
        out_shape=tuple(pltpu.VMEM(shape.shape, shape.dtype) for shape in shapes),
        in_specs=[pl.BlockSpec(memory_space=pltpu.SMEM)] + [hbm] * 9,
        out_specs=(vmem,) * 7,
        scratch_shapes=[
            pltpu.SMEM(hot_rows.shape, jnp.int32),
            pltpu.VMEM((rs, e), f32),
            pltpu.VMEM((rs, e), emb_grad.dtype),
            pltpu.VMEM((rs, e), f32),
            pltpu.VMEM((rs, e), f32),
            pltpu.VMEM((rs, e), f32),
            pltpu.VMEM((din, dout), f32),
            pltpu.VMEM((din, dout), f32),
            pltpu.VMEM((din, dout), f32),
            pltpu.VMEM((din, dout), f32),
            pltpu.VMEM((din, dout), WIRE),
            pltpu.VMEM((din, dout), f32),
            pltpu.VMEM((quads, piece, dout), WIRE),
            pltpu.VMEM((quads, piece, dout), WIRE),
            pltpu.VMEM((quads, piece, dout), WIRE),
            pltpu.VMEM((quads, piece, dout), WIRE),
            pltpu.VMEM((zs, piece, dout), WIRE),
            pltpu.VMEM((n_rows, 2, 8, e), f32),
            pltpu.VMEM((CORES * quads, 8, dout), f32),
            pltpu.VMEM((hot_n, e), f32),
            pltpu.VMEM((hot_n, e), f32),
            dma((4, chunks)),
            dma((5,)),
            dma((quads,)),
            dma((quads,)),
            dma((quads,)),
            dma((quads,)),
            dma((zs,)),
            dma((zs,)),
            dma((quads,)),
            dma((quads,)),
            dma((quads,)),
            dma((quads,)),
            dma((n_rows,)),
            dma((n_rows,)),
            dma((n_dp, hot_chunks)),
            dma((n_dp, hot_chunks)),
            dma((n_dp, hot_chunks)),
            dma((n_dp, hot_chunks)),
        ],
        compiler_params=pltpu.CompilerParams(
            collective_id=0, has_side_effects=True, vmem_limit_bytes=EXCHANGE_LIMIT
        ),
        name="exchange",
    )(
        block_counts,
        *(
            pltpu.with_memory_space_constraint(a, pltpu.HBM)
            for a in (
                hot_rows, emb_weight, emb_grad, emb_moment, emb_second,
                dense_grad, dense_weight, dense_moment, dense_second,
            )
        ),
    )
    return pl.pallas_call(
        functools.partial(write_out, len(shapes)),
        out_shape=shapes,
        in_specs=[vmem] * len(shapes),
        out_specs=(hbm,) * len(shapes),
        scratch_shapes=[dma((len(shapes),))],
        compiler_params=pltpu.CompilerParams(vmem_limit_bytes=WRITE_LIMIT),
        name="write_out",
    )(*outs)


def solution(mesh):
    in_specs = (
        P("dp", "rows", None),
        P("dp", "rows", None),
        P("dp", "rows", None),
        P("dp", "rows", None),
        P("dp", "rows", None),
        P("dp", "rows"),
        P(),
        P(("rows", "dp"), None, None),
        P(),
        P(),
    )
    out_specs = (
        P("dp", "rows", None),
        P("dp", "rows", None),
        P("dp", "rows", None),
        P(None, "rows", None, None),
        P(),
        P(),
        P(),
    )
    body = functools.partial(shards, mesh.shape["rows"], mesh.shape["dp"])
    return jax.shard_map(body, mesh=mesh, in_specs=in_specs, out_specs=out_specs, check_vma=False)
```
